32 devices in a mesh: hid: 8 (over y, x, core), tok: 4 (over z).
Axes of the slice: x: 2, y: 2, z: 4, core: 2. Of those that a mesh axis runs over, the one named last changes fastest.
Arguments:
- tokens: bfloat16 [896, 8192], P('tok', 'hid'), may hold values from -6 to 6
- in_blocks: bfloat16 [128, 6, 256, 256], P('hid', None, 'tok'), may hold values from -0.15625 to 0.15625
- in_left: bfloat16 [8192, 256], P(('hid', 'tok')), may hold values from -0.0625 to 0.0625
- in_right: bfloat16 [256, 32768], P(None, ('hid', 'tok')), may hold values from -0.375 to 0.375
- in_lists: int32 [128, 6], replicated, may hold values from 0 to 31, as said below
- out_blocks: bfloat16 [128, 6, 256, 256], P('hid', None, 'tok'), may hold values from -0.078125 to 0.078125
- out_left: bfloat16 [32768, 256], P(('hid', 'tok')), may hold values from -0.03125 to 0.03125
- out_right: bfloat16 [256, 8192], P(None, ('hid', 'tok')), may hold values from -0.375 to 0.375
- out_lists: int32 [128, 6], replicated, may hold values from 0 to 31, as said below
- cotangent: bfloat16 [896, 8192], P('tok', 'hid'), may hold values from -6 to 6
Outputs:
- layer_out: bfloat16 [896, 8192], P('tok', 'hid')
- grad_tokens: bfloat16 [896, 8192], P('tok', 'hid')
- grad_in_blocks: bfloat16 [128, 6, 256, 256], P('hid', None, 'tok')
- grad_in_left: bfloat16 [8192, 256], P(('hid', 'tok'))
- grad_in_right: bfloat16 [256, 32768], P(None, ('hid', 'tok'))
- grad_out_blocks: bfloat16 [128, 6, 256, 256], P('hid', None, 'tok')
- grad_out_left: bfloat16 [32768, 256], P(('hid', 'tok'))
- grad_out_right: bfloat16 [256, 8192], P(None, ('hid', 'tok'))
The draws below stay inside these ranges and needn't reach their ends.
Inputs may be any that keep to these rules, and one draw needn't show every extreme that they name: There is one whole number m, the same for every row, with in_lists[c, 0] = ((c * 8192) // 32768) XOR m, and in_lists[c, k] = in_lists[c, 0] XOR 2^(k-1) for k = 1 to 5. `out_lists`: the same butterfly form as in_lists, with its own number m, which differs from that of in_lists.
All inputs are finite; a program needn't handle non-finite values.
Results may differ from the reference program's by a relative error of at most 0.012.
Values may be sent and summed in bfloat16 or wider, within the bound.
A program may use at most 256 MiB of HBM per device.

```python
import jax
import jax.numpy as jnp
from jax import lax

D = 8192
FF = 32768
BLK = 256
LEVELS = 5
SLOTS = 6
RANK = 256
TOK_DEV = 224
TOKENS = 896
N_TOK = 4


def butterfly_codes(key):
    first_key, second_key = jax.random.split(key)
    code_one = jax.random.randint(first_key, (), 0, D // BLK, dtype=jnp.int32)
    offset = jax.random.randint(second_key, (), 1, D // BLK, dtype=jnp.int32)
    code_two = jnp.bitwise_xor(code_one, offset)
    return (code_one, code_two)


def butterfly_table(xor_code):
    hidden_ids = jnp.arange(FF // BLK, dtype=jnp.int32)
    base_ids = jnp.bitwise_xor(hidden_ids * D // FF, xor_code)
    powers = jnp.left_shift(jnp.ones((LEVELS,), jnp.int32), jnp.arange(LEVELS, dtype=jnp.int32))
    distances = jnp.concatenate([jnp.zeros((1,), jnp.int32), powers])
    return jnp.bitwise_xor(base_ids[:, None], distances[None, :]).astype(jnp.int32)


def draw_in_lists(key, part):
    code_one, code_two = butterfly_codes(jax.random.fold_in(key, 7))
    return butterfly_table(code_one)


def draw_out_lists(key, part):
    code_one, code_two = butterfly_codes(jax.random.fold_in(key, 7))
    return butterfly_table(code_two)


def block_scale(key, dims, cuts, low, high):
    factor_of, own = 1.0, jax.random.fold_in(key, 6)
    for axis_at, parts in cuts:
        heights = jnp.exp(jax.random.uniform(jax.random.fold_in(own, axis_at), (parts,), jnp.float32, low / len(cuts), high / len(cuts)))
        factor_of = factor_of * jnp.repeat(heights, dims[axis_at] // parts).reshape([-1 if axis == axis_at else 1 for axis in range(len(dims))])
    return factor_of


def bell_draw(key, extent, width, bound, cuts=(), kind=jnp.bfloat16):
    result = jax.random.normal(key, extent, jnp.float32) * width
    if len(cuts) > 0:
        result = block_scale(key, extent, cuts, -0.22, 0.18) * result
    return jnp.clip(result, min=-bound, max=bound).astype(kind)


def setup_inputs(seed: int = 0) -> dict:
    key_list = jax.random.split(jax.random.key(seed), 11)
    return {
        "tokens": bell_draw(key_list[0], (TOKENS, D), 1.0, 6.0, ((0, 4), (1, 8))),
        "in_blocks": bell_draw(key_list[1], (FF // BLK, SLOTS, BLK, BLK), (SLOTS * BLK) ** -0.5, 0.15625, ((0, 8), (2, 4))),
        "in_left": bell_draw(key_list[2], (D, RANK), D ** -0.5, 0.0625, ((0, 32),)),
        "in_right": bell_draw(key_list[3], (RANK, FF), RANK ** -0.5, 0.375, ((1, 32),)),
        "in_lists": draw_in_lists(jax.random.fold_in(key_list[10], 71), 0),
        "out_blocks": bell_draw(key_list[5], (FF // BLK, SLOTS, BLK, BLK), (4 * SLOTS * BLK) ** -0.5, 0.078125, ((0, 8), (2, 4))),
        "out_left": bell_draw(key_list[6], (FF, RANK), FF ** -0.5, 0.03125, ((0, 32),)),
        "out_right": bell_draw(key_list[7], (RANK, D), RANK ** -0.5, 0.375, ((1, 32),)),
        "out_lists": draw_out_lists(jax.random.fold_in(key_list[10], 71), 0),
        "cotangent": bell_draw(key_list[9], (TOKENS, D), 1.0, 6.0, ((0, 4), (1, 8))),
    }


def gelu_parts(preact):
    inner_coef = 0.7978845608028654
    cubic_coef = 0.044715
    inner_arg = inner_coef * (preact + cubic_coef * preact * preact * preact)
    tanh_val = jnp.tanh(inner_arg)
    active = 0.5 * preact * (1.0 + tanh_val)
    slopes = 0.5 * (1.0 + tanh_val) + 0.5 * preact * (1.0 - tanh_val * tanh_val) * inner_coef * (1.0 + 3.0 * cubic_coef * preact * preact)
    return (active, slopes)

def dot_rows(left_arr, right_arr):
    return lax.dot_general(left_arr, right_arr, (((0,), (0,)), ((), ())), preferred_element_type=jnp.float32)

def dot_cols(left_arr, right_arr):
    return lax.dot_general(left_arr, right_arr, (((1,), (1,)), ((), ())), preferred_element_type=jnp.float32)

def rounded(values):
    return lax.optimization_barrier(values.astype(jnp.bfloat16)).astype(jnp.float32)

def reference(tokens, in_blocks, in_left, in_right, in_lists, out_blocks, out_left, out_right, out_lists, cotangent):
    in_count = D // BLK
    hid_count = FF // BLK
    loss_scale = lax.rsqrt(jnp.float32(TOKENS))
    pick_in = (in_lists.T[:, :, None] == jnp.arange(in_count, dtype=jnp.int32)[None, None, :]).astype(jnp.float32)
    pick_out = (out_lists.T[:, :, None] == jnp.arange(in_count, dtype=jnp.int32)[None, None, :]).astype(jnp.float32)
    first_w = in_blocks.astype(jnp.float32)
    second_w = out_blocks.astype(jnp.float32)

    def one_group(running, pieces):
        tok_group, cot_group = pieces
        row_count = tok_group.shape[0]
        low_in = jnp.dot(tok_group, in_left, preferred_element_type=jnp.float32).astype(jnp.bfloat16)
        low_back = dot_cols(cot_group, out_right).astype(jnp.bfloat16)
        gathered = tok_group.reshape(row_count, in_count, BLK)[:, in_lists.T].astype(jnp.float32)
        preact = jnp.einsum('nshb,hsbf->nhf', gathered, first_w).reshape(row_count, FF)
        preact = preact + jnp.dot(low_in, in_right, preferred_element_type=jnp.float32)
        active, slopes = gelu_parts(preact)
        hidden = active.astype(jnp.bfloat16)
        low_mid = jnp.dot(hidden, out_left, preferred_element_type=jnp.float32).astype(jnp.bfloat16)
        hidden_f = hidden.astype(jnp.float32).reshape(row_count, hid_count, BLK)
        out_parts = jnp.einsum('nhf,hsfo->nsho', hidden_f, second_w)
        sparse_out = jnp.einsum('nsho,shc->nco', out_parts, pick_out, precision=lax.Precision.HIGHEST).reshape(row_count, D)
        layer_out = (sparse_out + jnp.dot(low_mid, out_right, preferred_element_type=jnp.float32)).astype(jnp.bfloat16)
        grad_in = cot_group.reshape(row_count, in_count, BLK)[:, out_lists.T].astype(jnp.float32)
        grad_hidden = jnp.einsum('nsho,hsfo->nhf', grad_in, second_w).reshape(row_count, FF)
        grad_hidden = grad_hidden + dot_cols(low_back, out_left)
        grad_pre = (grad_hidden * slopes).astype(jnp.bfloat16)
        low_grad = dot_cols(grad_pre, in_right).astype(jnp.bfloat16)
        grad_pre_f = grad_pre.astype(jnp.float32).reshape(row_count, hid_count, BLK)
        back_parts = jnp.einsum('nhf,hsbf->nshb', grad_pre_f, first_w)
        sparse_back = jnp.einsum('nshb,shc->ncb', back_parts, pick_in, precision=lax.Precision.HIGHEST).reshape(row_count, D)
        grad_tokens = (sparse_back + dot_cols(low_grad, in_left)).astype(jnp.bfloat16)
        terms = (rounded(loss_scale * jnp.einsum('nshb,nhf->hsbf', gathered, grad_pre_f)), rounded(loss_scale * jnp.einsum('nhf,nsho->hsfo', hidden_f, grad_in)), rounded(loss_scale * dot_rows(tok_group, low_grad)), rounded(loss_scale * dot_rows(low_in, grad_pre)), rounded(loss_scale * dot_rows(hidden, low_back)), rounded(loss_scale * dot_rows(low_mid, cot_group)))
        running = tuple((acc_val + new_val for acc_val, new_val in zip(running, terms)))
        return (running, (layer_out, grad_tokens))
    zero_sums = (jnp.zeros(in_blocks.shape, jnp.float32), jnp.zeros(out_blocks.shape, jnp.float32), jnp.zeros(in_left.shape, jnp.float32), jnp.zeros(in_right.shape, jnp.float32), jnp.zeros(out_left.shape, jnp.float32), jnp.zeros(out_right.shape, jnp.float32))
    grouped = (tokens.reshape(N_TOK, TOK_DEV, D), cotangent.reshape(N_TOK, TOK_DEV, D))
    sums, (outs_all, grads_all) = lax.scan(one_group, zero_sums, grouped)
    return (outs_all.reshape(TOKENS, D), grads_all.reshape(TOKENS, D), sums[0].astype(jnp.bfloat16), sums[2].astype(jnp.bfloat16), sums[3].astype(jnp.bfloat16), sums[1].astype(jnp.bfloat16), sums[4].astype(jnp.bfloat16), sums[5].astype(jnp.bfloat16))
```

```python
import jax
import jax.numpy as jnp
from jax import lax
from jax.sharding import PartitionSpec as P

D = 8192
BLK = 256


def gelu_parts(preact):
    inner_coef = 0.7978845608028654
    cubic_coef = 0.044715
    inner_arg = inner_coef * (preact + cubic_coef * preact * preact * preact)
    tanh_val = jnp.tanh(inner_arg)
    active = 0.5 * preact * (1.0 + tanh_val)
    slopes = 0.5 * (1.0 + tanh_val) + 0.5 * preact * (1.0 - tanh_val * tanh_val) * inner_coef * (
        1.0 + 3.0 * cubic_coef * preact * preact
    )
    return (active, slopes)


def dot_rows(left_arr, right_arr):
    return lax.dot_general(
        left_arr, right_arr, (((0,), (0,)), ((), ())), preferred_element_type=jnp.float32
    )


def dot_cols(left_arr, right_arr):
    return lax.dot_general(
        left_arr, right_arr, (((1,), (1,)), ((), ())), preferred_element_type=jnp.float32
    )


def rank_sum(values):
    return lax.psum(values, "hid")


def own_lists(lists, hid_blocks):
    return lax.dynamic_slice_in_dim(lists, lax.axis_index("hid") * hid_blocks, hid_blocks, 0)


def gather_in(values, lists, hid_blocks, blk_width):
    whole = lax.all_gather(values, "hid", axis=1, tiled=True)
    mine = own_lists(lists, hid_blocks)
    blocks = whole.reshape(whole.shape[0], whole.shape[1] // blk_width, blk_width)
    return blocks[:, mine.T]


def scatter_out(parts, lists, hid_blocks):
    mine = own_lists(lists, hid_blocks)
    picker = (mine.T[:, :, None] == jnp.arange(D // BLK, dtype=jnp.int32)[None, None, :]).astype(
        jnp.float32
    )
    dense = jnp.einsum("nsho,shc->nco", parts, picker, precision=lax.Precision.HIGHEST)
    return lax.psum_scatter(
        dense.reshape(dense.shape[0], -1), "hid", scatter_dimension=1, tiled=True
    )


def route_in(values, lists, hid_blocks, blk_width):
    return gather_in(values, lists, hid_blocks, blk_width)


def route_out(parts, lists, hid_blocks):
    return scatter_out(parts, lists, hid_blocks)


def local_gathered(
    tokens,
    in_blocks,
    in_left,
    in_right,
    in_lists,
    out_blocks,
    out_left,
    out_right,
    out_lists,
    cotangent,
):
    row_count, col_span = tokens.shape
    hid_blocks = in_blocks.shape[0]
    slot_count = in_blocks.shape[1]
    blk_width = in_blocks.shape[3]
    tok_count = lax.axis_size("tok")
    w_first, w_second, left_one, right_one, left_two, right_two = (
        lax.all_gather(in_blocks, "tok", axis=2, tiled=True),
        lax.all_gather(out_blocks, "tok", axis=2, tiled=True),
        lax.all_gather(in_left, "tok", axis=0, tiled=True),
        lax.all_gather(in_right, "tok", axis=1, tiled=True),
        lax.all_gather(out_left, "tok", axis=0, tiled=True),
        lax.all_gather(out_right, "tok", axis=1, tiled=True),
    )
    low_in, low_back = rank_sum(
        (
            jnp.dot(tokens, left_one, preferred_element_type=jnp.float32),
            dot_cols(cotangent, right_two),
        )
    )
    low_in = low_in.astype(jnp.bfloat16)
    low_back = low_back.astype(jnp.bfloat16)
    gathered = route_in(tokens, in_lists, hid_blocks, blk_width)
    group_count = gathered.shape[2]
    per_group = hid_blocks // group_count
    first_r = w_first.reshape(group_count, per_group, slot_count, blk_width, blk_width)
    second_r = w_second.reshape(group_count, per_group, slot_count, blk_width, blk_width)
    preact = jnp.einsum(
        "nseb,eqsbf->neqf", gathered, first_r, preferred_element_type=jnp.float32
    ).reshape(row_count, -1)
    preact = preact + jnp.dot(low_in, right_one, preferred_element_type=jnp.float32)
    active, slopes = gelu_parts(preact)
    hidden = active.astype(jnp.bfloat16)
    low_mid = rank_sum(jnp.dot(hidden, left_two, preferred_element_type=jnp.float32)).astype(
        jnp.bfloat16
    )
    hidden_r = hidden.reshape(row_count, group_count, per_group, blk_width)
    out_parts = jnp.einsum(
        "neqf,eqsfo->nseo", hidden_r, second_r, preferred_element_type=jnp.float32
    )
    sparse_out = route_out(out_parts, out_lists, hid_blocks)
    layer_out = (
        sparse_out + jnp.dot(low_mid, right_two, preferred_element_type=jnp.float32)
    ).astype(jnp.bfloat16)
    grad_in = route_in(cotangent, out_lists, hid_blocks, blk_width)
    grad_hidden = jnp.einsum(
        "nseo,eqsfo->neqf", grad_in, second_r, preferred_element_type=jnp.float32
    ).reshape(row_count, -1)
    grad_hidden = grad_hidden + dot_cols(low_back, left_two)
    grad_pre = (grad_hidden * slopes).astype(jnp.bfloat16)
    low_grad = rank_sum(dot_cols(grad_pre, right_one)).astype(jnp.bfloat16)
    grad_pre_r = grad_pre.reshape(row_count, group_count, per_group, blk_width)
    back_parts = jnp.einsum(
        "neqf,eqsbf->nseb", grad_pre_r, first_r, preferred_element_type=jnp.float32
    )
    sparse_back = route_out(back_parts, in_lists, hid_blocks)
    grad_tokens = (sparse_back + dot_cols(low_grad, left_one)).astype(jnp.bfloat16)
    loss_scale = lax.rsqrt(jnp.float32(row_count * tok_count))
    terms = (
        loss_scale
        * jnp.einsum(
            "nseb,neqf->eqsbf", gathered, grad_pre_r, preferred_element_type=jnp.float32
        ).reshape(w_first.shape),
        loss_scale
        * jnp.einsum(
            "neqf,nseo->eqsfo", hidden_r, grad_in, preferred_element_type=jnp.float32
        ).reshape(w_second.shape),
        loss_scale * dot_rows(tokens, low_grad),
        loss_scale * dot_rows(low_in, grad_pre),
        loss_scale * dot_rows(hidden, low_back),
        loss_scale * dot_rows(low_mid, cotangent),
    )
    shares = (
        lax.psum_scatter(
            terms[0].astype(jnp.bfloat16), "tok", scatter_dimension=2, tiled=True
        ).astype(jnp.float32),
        lax.psum_scatter(
            terms[1].astype(jnp.bfloat16), "tok", scatter_dimension=2, tiled=True
        ).astype(jnp.float32),
        lax.psum_scatter(
            terms[2].astype(jnp.bfloat16), "tok", scatter_dimension=0, tiled=True
        ).astype(jnp.float32),
        lax.psum_scatter(
            terms[3].astype(jnp.bfloat16), "tok", scatter_dimension=1, tiled=True
        ).astype(jnp.float32),
        lax.psum_scatter(
            terms[4].astype(jnp.bfloat16), "tok", scatter_dimension=0, tiled=True
        ).astype(jnp.float32),
        lax.psum_scatter(
            terms[5].astype(jnp.bfloat16), "tok", scatter_dimension=1, tiled=True
        ).astype(jnp.float32),
    )
    return (
        layer_out,
        grad_tokens,
        shares[0].astype(jnp.bfloat16),
        shares[2].astype(jnp.bfloat16),
        shares[3].astype(jnp.bfloat16),
        shares[1].astype(jnp.bfloat16),
        shares[4].astype(jnp.bfloat16),
        shares[5].astype(jnp.bfloat16),
    )


def swap_tok(pieces):
    count = lax.axis_size("tok")
    return [
        piece
        if dist == 0
        else lax.ppermute(piece, "tok", [(src, src ^ dist) for src in range(count)])
        for dist, piece in enumerate(pieces)
    ]


def swap_hid(values, dist):
    count = lax.axis_size("hid")
    return lax.ppermute(values, "hid", [(src, src ^ dist) for src in range(count)])


def in_group_shifts(count):
    return [0] + [1 << bit for bit in range(count.bit_length() - 1)]


def hid_shifts(count):
    return [1 << bit for bit in range(count.bit_length() - 1)]


def column_block(values, index, blk_width):
    return lax.dynamic_slice_in_dim(
        values, index * blk_width, blk_width, values.ndim - 1
    )


def fetch_slots(values, code, blk_width):
    n_tok = lax.axis_size("tok")
    n_hid = lax.axis_size("hid")
    me_tok = lax.axis_index("tok")
    me_hid = lax.axis_index("hid")
    whole = lax.all_gather(values, "hid", axis=0, tiled=False)
    group = lax.dynamic_index_in_dim(whole, me_hid ^ (code // n_tok), 0, keepdims=False)
    shifts = in_group_shifts(n_tok)
    pieces = [
        jnp.stack(
            [
                column_block(group, me_tok ^ dist ^ (code % n_tok) ^ shift, blk_width)
                for shift in shifts
            ]
        )
        for dist in range(n_tok)
    ]
    got = jnp.concatenate(swap_tok(pieces), axis=1)
    slots = [got[pos] for pos in range(len(shifts))]
    slots += [swap_hid(slots[0], dist) for dist in hid_shifts(n_hid)]
    return jnp.concatenate(slots, axis=1)


def return_slots(parts, code, rows, blk_width):
    n_tok = lax.axis_size("tok")
    n_hid = lax.axis_size("hid")
    me_tok = lax.axis_index("tok")
    me_hid = lax.axis_index("hid")
    shifts = in_group_shifts(n_tok)
    base = parts[:, :blk_width]
    for pos, dist in enumerate(hid_shifts(n_hid)):
        at = (len(shifts) + pos) * blk_width
        moved = swap_hid(parts[:, at : at + blk_width].astype(jnp.bfloat16), dist)
        base = base + moved.astype(jnp.float32)
    kept = jnp.stack(
        [base.astype(jnp.bfloat16)]
        + [
            parts[:, pos * blk_width : (pos + 1) * blk_width].astype(jnp.bfloat16)
            for pos in range(1, len(shifts))
        ]
    )
    got = swap_tok([kept[:, dist * rows : (dist + 1) * rows] for dist in range(n_tok)])
    sums = []
    for place in range(n_tok):
        total = 0.0
        for pos, shift in enumerate(shifts):
            total = total + got[place ^ shift][pos].astype(jnp.float32)
        sums.append(total.astype(jnp.bfloat16))
    whole = lax.all_gather(jnp.stack(sums), "hid", axis=0, tiled=False)
    group = lax.dynamic_index_in_dim(whole, me_hid ^ (code // n_tok), 0, keepdims=False)
    return jnp.concatenate(
        [
            lax.dynamic_index_in_dim(
                group, me_tok ^ (code % n_tok) ^ place, 0, keepdims=False
            )
            for place in range(n_tok)
        ],
        axis=1,
    )


def gather_weights(blocks):
    n_tok = lax.axis_size("tok")
    me_tok = lax.axis_index("tok")
    per = blocks.shape[0] // n_tok
    deep = blocks.shape[2]
    got = swap_tok(
        [
            lax.dynamic_slice_in_dim(blocks, (me_tok ^ dist) * per, per, 0)
            for dist in range(n_tok)
        ]
    )
    whole = jnp.zeros((per, blocks.shape[1], deep * n_tok, blocks.shape[3]), blocks.dtype)
    for dist in range(n_tok):
        whole = lax.dynamic_update_slice_in_dim(whole, got[dist], (me_tok ^ dist) * deep, 2)
    return whole


def scatter_weights(whole):
    n_tok = lax.axis_size("tok")
    me_tok = lax.axis_index("tok")
    per = whole.shape[0]
    deep = whole.shape[2] // n_tok
    got = swap_tok(
        [
            lax.dynamic_slice_in_dim(whole, (me_tok ^ dist) * deep, deep, 2)
            for dist in range(n_tok)
        ]
    )
    blocks = jnp.zeros((per * n_tok, whole.shape[1], deep, whole.shape[3]), whole.dtype)
    for dist in range(n_tok):
        blocks = lax.dynamic_update_slice_in_dim(blocks, got[dist], (me_tok ^ dist) * per, 0)
    return blocks


def own_columns(values, blk_width):
    n_tok = lax.axis_size("tok")
    me_tok = lax.axis_index("tok")
    return jnp.concatenate(
        swap_tok([column_block(values, me_tok ^ dist, blk_width) for dist in range(n_tok)]),
        axis=0,
    )


def local_moved(
    tokens,
    in_blocks,
    in_left,
    in_right,
    in_lists,
    out_blocks,
    out_left,
    out_right,
    out_lists,
    cotangent,
):
    rows = tokens.shape[0]
    slots = in_blocks.shape[1]
    blk = in_blocks.shape[3]
    n_tok = lax.axis_size("tok")
    per = in_blocks.shape[0] // n_tok
    rank = in_left.shape[1]
    code_in = in_lists[0, 0]
    code_out = out_lists[0, 0]
    left_one = lax.all_gather(in_left, "tok", axis=0, tiled=True)
    right_two = lax.all_gather(out_right, "tok", axis=1, tiled=True)
    own_in, own_back = rank_sum(
        (
            jnp.dot(tokens, left_one, preferred_element_type=jnp.float32),
            dot_cols(cotangent, right_two),
        )
    )
    own_low = jnp.concatenate(
        [own_in.astype(jnp.bfloat16), own_back.astype(jnp.bfloat16)], axis=1
    )
    low_all = jnp.concatenate(swap_tok([own_low] * n_tok), axis=0)
    low_in = low_all[:, :rank]
    low_back = low_all[:, rank:]
    x_in = fetch_slots(tokens, code_in, blk)
    x_cot = fetch_slots(cotangent, code_out, blk)
    tok_own = own_columns(tokens, blk)
    cot_own = own_columns(cotangent, blk)
    first = gather_weights(in_blocks).reshape(per, slots * blk, blk)
    second = gather_weights(out_blocks)

    preact = jnp.concatenate(
        [jnp.dot(x_in, first[at], preferred_element_type=jnp.float32) for at in range(per)],
        axis=1,
    ) + jnp.dot(low_in, in_right, preferred_element_type=jnp.float32)
    active, slopes = gelu_parts(preact)
    hidden = active.astype(jnp.bfloat16)
    hidden_q = [hidden[:, at * blk : (at + 1) * blk] for at in range(per)]
    grad_hidden = jnp.concatenate(
        [
            sum(
                dot_cols(x_cot[:, k * blk : (k + 1) * blk], second[at, k])
                for k in range(slots)
            )
            for at in range(per)
        ],
        axis=1,
    ) + dot_cols(low_back, out_left)
    grad_pre = (grad_hidden * slopes).astype(jnp.bfloat16)
    grad_q = [grad_pre[:, at * blk : (at + 1) * blk] for at in range(per)]

    low_parts = jnp.concatenate(
        [
            jnp.dot(hidden, out_left, preferred_element_type=jnp.float32),
            dot_cols(grad_pre, in_right),
        ],
        axis=1,
    ).astype(jnp.bfloat16)
    low_got = swap_tok([low_parts[d * rows : (d + 1) * rows] for d in range(n_tok)])
    low_sum = rank_sum(sum(piece.astype(jnp.float32) for piece in low_got)).astype(
        jnp.bfloat16
    )
    low_mid = low_sum[:, :rank]
    low_grad = low_sum[:, rank:]
    low_sum_all = jnp.concatenate(swap_tok([low_sum] * n_tok), axis=0)

    out_parts = jnp.concatenate(
        [
            sum(
                jnp.dot(hidden_q[at], second[at, k], preferred_element_type=jnp.float32)
                for at in range(per)
            )
            for k in range(slots)
        ],
        axis=1,
    )
    back_parts = sum(dot_cols(grad_q[at], first[at]) for at in range(per))
    sparse_out = return_slots(out_parts, code_out, rows, blk)
    sparse_back = return_slots(back_parts, code_in, rows, blk)
    layer_out = (
        sparse_out.astype(jnp.float32)
        + jnp.dot(low_mid, right_two, preferred_element_type=jnp.float32)
    ).astype(jnp.bfloat16)
    grad_tokens = (sparse_back.astype(jnp.float32) + dot_cols(low_grad, left_one)).astype(
        jnp.bfloat16
    )

    scale = lax.rsqrt(jnp.float32(rows * n_tok))
    grad_first = jnp.stack(
        [(scale * dot_rows(x_in, grad_q[at])).astype(jnp.bfloat16) for at in range(per)]
    ).reshape(per, slots, blk, blk)
    grad_second = jnp.stack(
        [
            jnp.stack(
                [
                    (scale * dot_rows(hidden_q[at], x_cot[:, k * blk : (k + 1) * blk])).astype(
                        jnp.bfloat16
                    )
                    for k in range(slots)
                ]
            )
            for at in range(per)
        ]
    )
    return (
        layer_out,
        grad_tokens,
        scatter_weights(grad_first),
        (scale * dot_rows(tok_own, low_sum_all[:, rank:])).astype(jnp.bfloat16),
        (scale * dot_rows(low_in, grad_pre)).astype(jnp.bfloat16),
        scatter_weights(grad_second),
        (scale * dot_rows(hidden, low_back)).astype(jnp.bfloat16),
        (scale * dot_rows(low_sum_all[:, :rank], cot_own)).astype(jnp.bfloat16),
    )


def power_of_two(count):
    return count & (count - 1) == 0


def local(*arrays):
    tokens, in_blocks = arrays[0], arrays[1]
    n_tok = lax.axis_size("tok")
    n_hid = lax.axis_size("hid")
    whole_groups = (
        power_of_two(n_tok)
        and power_of_two(n_hid)
        and tokens.shape[1] == n_tok * in_blocks.shape[3]
        and in_blocks.shape[0] % n_tok == 0
    )
    return local_moved(*arrays) if whole_groups else local_gathered(*arrays)


def solution(mesh):
    return jax.shard_map(
        local,
        mesh=mesh,
        in_specs=(
            P("tok", "hid"),
            P("hid", None, "tok", None),
            P(("hid", "tok"), None),
            P(None, ("hid", "tok")),
            P(),
            P("hid", None, "tok", None),
            P(("hid", "tok"), None),
            P(None, ("hid", "tok")),
            P(),
            P("tok", "hid"),
        ),
        out_specs=(
            P("tok", "hid"),
            P("tok", "hid"),
            P("hid", None, "tok", None),
            P(("hid", "tok"), None),
            P(None, ("hid", "tok")),
            P("hid", None, "tok", None),
            P(("hid", "tok"), None),
            P(None, ("hid", "tok")),
        ),
        check_vma=False,
    )
```

```python
import jax
import jax.numpy as jnp
from jax import lax
from jax.experimental import pallas as pl
from jax.experimental.pallas import tpu as pltpu
from jax.sharding import PartitionSpec as P

D = 8192
BLK = 256


def gelu_parts(preact):
    inner_coef = 0.7978845608028654
    cubic_coef = 0.044715
    inner_arg = inner_coef * (preact + cubic_coef * preact * preact * preact)
    tanh_val = jnp.tanh(inner_arg)
    active = 0.5 * preact * (1.0 + tanh_val)
    slopes = 0.5 * (1.0 + tanh_val) + 0.5 * preact * (1.0 - tanh_val * tanh_val) * inner_coef * (
        1.0 + 3.0 * cubic_coef * preact * preact
    )
    return (active, slopes)


def dot_rows(left_arr, right_arr):
    return lax.dot_general(
        left_arr, right_arr, (((0,), (0,)), ((), ())), preferred_element_type=jnp.float32
    )


def dot_cols(left_arr, right_arr):
    return lax.dot_general(
        left_arr, right_arr, (((1,), (1,)), ((), ())), preferred_element_type=jnp.float32
    )


def rank_sum(values):
    return lax.psum(values, "hid")


def own_lists(lists, hid_blocks):
    return lax.dynamic_slice_in_dim(lists, lax.axis_index("hid") * hid_blocks, hid_blocks, 0)


def gather_in(values, lists, hid_blocks, blk_width):
    whole = lax.all_gather(values, "hid", axis=1, tiled=True)
    mine = own_lists(lists, hid_blocks)
    blocks = whole.reshape(whole.shape[0], whole.shape[1] // blk_width, blk_width)
    return blocks[:, mine.T]


def scatter_out(parts, lists, hid_blocks):
    mine = own_lists(lists, hid_blocks)
    picker = (mine.T[:, :, None] == jnp.arange(D // BLK, dtype=jnp.int32)[None, None, :]).astype(
        jnp.float32
    )
    dense = jnp.einsum("nsho,shc->nco", parts, picker, precision=lax.Precision.HIGHEST)
    return lax.psum_scatter(
        dense.reshape(dense.shape[0], -1), "hid", scatter_dimension=1, tiled=True
    )


def route_in(values, lists, hid_blocks, blk_width):
    return gather_in(values, lists, hid_blocks, blk_width)


def route_out(parts, lists, hid_blocks):
    return scatter_out(parts, lists, hid_blocks)


def local_gathered(
    tokens,
    in_blocks,
    in_left,
    in_right,
    in_lists,
    out_blocks,
    out_left,
    out_right,
    out_lists,
    cotangent,
):
    row_count, col_span = tokens.shape
    hid_blocks = in_blocks.shape[0]
    slot_count = in_blocks.shape[1]
    blk_width = in_blocks.shape[3]
    tok_count = lax.axis_size("tok")
    w_first, w_second, left_one, right_one, left_two, right_two = (
        lax.all_gather(in_blocks, "tok", axis=2, tiled=True),
        lax.all_gather(out_blocks, "tok", axis=2, tiled=True),
        lax.all_gather(in_left, "tok", axis=0, tiled=True),
        lax.all_gather(in_right, "tok", axis=1, tiled=True),
        lax.all_gather(out_left, "tok", axis=0, tiled=True),
        lax.all_gather(out_right, "tok", axis=1, tiled=True),
    )
    low_in, low_back = rank_sum(
        (
            jnp.dot(tokens, left_one, preferred_element_type=jnp.float32),
            dot_cols(cotangent, right_two),
        )
    )
    low_in = low_in.astype(jnp.bfloat16)
    low_back = low_back.astype(jnp.bfloat16)
    gathered = route_in(tokens, in_lists, hid_blocks, blk_width)
    group_count = gathered.shape[2]
    per_group = hid_blocks // group_count
    first_r = w_first.reshape(group_count, per_group, slot_count, blk_width, blk_width)
    second_r = w_second.reshape(group_count, per_group, slot_count, blk_width, blk_width)
    preact = jnp.einsum(
        "nseb,eqsbf->neqf", gathered, first_r, preferred_element_type=jnp.float32
    ).reshape(row_count, -1)
    preact = preact + jnp.dot(low_in, right_one, preferred_element_type=jnp.float32)
    active, slopes = gelu_parts(preact)
    hidden = active.astype(jnp.bfloat16)
    low_mid = rank_sum(jnp.dot(hidden, left_two, preferred_element_type=jnp.float32)).astype(
        jnp.bfloat16
    )
    hidden_r = hidden.reshape(row_count, group_count, per_group, blk_width)
    out_parts = jnp.einsum(
        "neqf,eqsfo->nseo", hidden_r, second_r, preferred_element_type=jnp.float32
    )
    sparse_out = route_out(out_parts, out_lists, hid_blocks)
    layer_out = (
        sparse_out + jnp.dot(low_mid, right_two, preferred_element_type=jnp.float32)
    ).astype(jnp.bfloat16)
    grad_in = route_in(cotangent, out_lists, hid_blocks, blk_width)
    grad_hidden = jnp.einsum(
        "nseo,eqsfo->neqf", grad_in, second_r, preferred_element_type=jnp.float32
    ).reshape(row_count, -1)
    grad_hidden = grad_hidden + dot_cols(low_back, left_two)
    grad_pre = (grad_hidden * slopes).astype(jnp.bfloat16)
    low_grad = rank_sum(dot_cols(grad_pre, right_one)).astype(jnp.bfloat16)
    grad_pre_r = grad_pre.reshape(row_count, group_count, per_group, blk_width)
    back_parts = jnp.einsum(
        "neqf,eqsbf->nseb", grad_pre_r, first_r, preferred_element_type=jnp.float32
    )
    sparse_back = route_out(back_parts, in_lists, hid_blocks)
    grad_tokens = (sparse_back + dot_cols(low_grad, left_one)).astype(jnp.bfloat16)
    loss_scale = lax.rsqrt(jnp.float32(row_count * tok_count))
    terms = (
        loss_scale
        * jnp.einsum(
            "nseb,neqf->eqsbf", gathered, grad_pre_r, preferred_element_type=jnp.float32
        ).reshape(w_first.shape),
        loss_scale
        * jnp.einsum(
            "neqf,nseo->eqsfo", hidden_r, grad_in, preferred_element_type=jnp.float32
        ).reshape(w_second.shape),
        loss_scale * dot_rows(tokens, low_grad),
        loss_scale * dot_rows(low_in, grad_pre),
        loss_scale * dot_rows(hidden, low_back),
        loss_scale * dot_rows(low_mid, cotangent),
    )
    shares = (
        lax.psum_scatter(
            terms[0].astype(jnp.bfloat16), "tok", scatter_dimension=2, tiled=True
        ).astype(jnp.float32),
        lax.psum_scatter(
            terms[1].astype(jnp.bfloat16), "tok", scatter_dimension=2, tiled=True
        ).astype(jnp.float32),
        lax.psum_scatter(
            terms[2].astype(jnp.bfloat16), "tok", scatter_dimension=0, tiled=True
        ).astype(jnp.float32),
        lax.psum_scatter(
            terms[3].astype(jnp.bfloat16), "tok", scatter_dimension=1, tiled=True
        ).astype(jnp.float32),
        lax.psum_scatter(
            terms[4].astype(jnp.bfloat16), "tok", scatter_dimension=0, tiled=True
        ).astype(jnp.float32),
        lax.psum_scatter(
            terms[5].astype(jnp.bfloat16), "tok", scatter_dimension=1, tiled=True
        ).astype(jnp.float32),
    )
    return (
        layer_out,
        grad_tokens,
        shares[0].astype(jnp.bfloat16),
        shares[2].astype(jnp.bfloat16),
        shares[3].astype(jnp.bfloat16),
        shares[1].astype(jnp.bfloat16),
        shares[4].astype(jnp.bfloat16),
        shares[5].astype(jnp.bfloat16),
    )


def in_group_shifts(count):
    return [0] + [1 << bit for bit in range(count.bit_length() - 1)]


def hid_shifts(count):
    return [1 << bit for bit in range(count.bit_length() - 1)]


def span(index, size):
    return pl.ds(pl.multiple_of(index * size, size), size)


def greet(partners):
    me_tok, me_hid = lax.axis_index("tok"), lax.axis_index("hid")
    barrier = pltpu.get_barrier_semaphore()
    for tok_dist, hid_dist in partners:
        pl.semaphore_signal(
            barrier,
            inc=1,
            device_id={"hid": me_hid ^ hid_dist, "tok": me_tok ^ tok_dist},
            device_id_type=pl.DeviceIdType.MESH,
        )
    pl.semaphore_wait(barrier, len(partners))


class Mover:
    def __init__(self, send, recv):
        self.send, self.recv, self.used = send, recv, 0
        self.open_copies = []

    def start(self, src, dst, tok_dist=0, hid_dist=0):
        at = self.used
        self.used += 1
        if tok_dist == 0 and hid_dist == 0:
            copy = pltpu.make_async_copy(src, dst, self.recv.at[at])
            copy.start()
            entry = [copy, True, False]
        else:
            copy = pltpu.make_async_remote_copy(
                src_ref=src,
                dst_ref=dst,
                send_sem=self.send.at[at],
                recv_sem=self.recv.at[at],
                device_id={
                    "hid": lax.axis_index("hid") ^ hid_dist,
                    "tok": lax.axis_index("tok") ^ tok_dist,
                },
                device_id_type=pl.DeviceIdType.MESH,
            )
            copy.start()
            entry = [copy, False, False]
        self.open_copies.append(entry)
        return entry

    def arrived(self, entry):
        if not entry[2]:
            if entry[1]:
                entry[0].wait()
            else:
                entry[0].wait_recv()
            entry[2] = True

    def finish(self):
        for entry in self.open_copies:
            self.arrived(entry)
        for entry in self.open_copies:
            if not entry[1]:
                entry[0].wait_send()


def run_exchange(body, inputs, shapes, copies, ident, in_space=pl.ANY, scratch=()):
    any_spec = pl.BlockSpec(memory_space=pl.ANY)
    return pl.pallas_call(
        body,
        out_shape=[jax.ShapeDtypeStruct(shape, jnp.bfloat16) for shape in shapes],
        in_specs=[pl.BlockSpec(memory_space=in_space)] * len(inputs),
        out_specs=[any_spec] * len(shapes),
        scratch_shapes=[
            pltpu.SemaphoreType.DMA((copies,)),
            pltpu.SemaphoreType.DMA((copies,)),
            *scratch,
        ],
        compiler_params=pltpu.CompilerParams(collective_id=ident, has_side_effects=True),
        cost_estimate=pl.CostEstimate(
            flops=0, bytes_accessed=200_000_000, transcendentals=0
        ),
    )(*inputs)


def weights_in(tokens, cotangent, in_left, out_right, in_blocks, out_blocks):
    n_tok = lax.axis_size("tok")
    rows, blk = tokens.shape[0], in_blocks.shape[3]
    hid_blocks, slots, deep, _ = in_blocks.shape
    per = hid_blocks // n_tok
    rank = in_left.shape[1]

    def body(tok, cot, left, right, first, second, left_o, right_o, tok_o, cot_o, f_o, s_o, send, recv):
        me = lax.axis_index("tok")
        greet([(dist, 0) for dist in range(1, n_tok)])
        mover = Mover(send, recv)
        for dist in range(n_tok):
            mover.start(left, left_o.at[span(me, blk), :], dist)
            mover.start(right, right_o.at[:, span(me, blk)], dist)
        for dist in list(range(1, n_tok)) + [0]:
            for src, dst in ((first, f_o), (second, s_o)):
                mover.start(
                    src.at[span(me ^ dist, per)],
                    dst.at[:, :, span(me, deep), :],
                    dist,
                )
        for dist in range(n_tok):
            for src, dst in ((tok, tok_o), (cot, cot_o)):
                mover.start(
                    src.at[:, span(me ^ dist, blk)], dst.at[pl.ds(dist * rows, rows), :], dist
                )
        mover.finish()

    full = (per, slots, deep * n_tok, blk)
    return run_exchange(
        body,
        (tokens, cotangent, in_left, out_right, in_blocks, out_blocks),
        [
            (blk * n_tok, rank),
            (rank, blk * n_tok),
            (rows * n_tok, blk),
            (rows * n_tok, blk),
            full,
            full,
        ],
        6 * n_tok,
        1,
    )


def slots_in(low, group_in, group_cot, blk):
    n_tok, n_hid = lax.axis_size("tok"), lax.axis_size("hid")
    rows = low.shape[0]
    near, far = in_group_shifts(n_tok), hid_shifts(n_hid)
    width = (len(near) + len(far)) * blk

    def body(low_i, in_i, cot_i, low_o, in_o, cot_o, send, recv):
        me = lax.axis_index("tok")
        greet(
            [(dist, 0) for dist in range(1, n_tok)] + [(0, dist) for dist in far]
        )
        mover = Mover(send, recv)
        pairs = ((in_i, in_o), (cot_i, cot_o))
        base = []
        for pos, shift in enumerate(near):
            for dist in range(n_tok):
                for src, dst in pairs:
                    entry = mover.start(
                        src.at[:, span(me ^ dist ^ shift, blk)],
                        dst.at[pl.ds(dist * rows, rows), pl.ds(pos * blk, blk)],
                        dist,
                    )
                    if pos == 0:
                        base.append((entry, dist, dst))
        for dist in range(n_tok):
            mover.start(low_i, low_o.at[pl.ds(dist * rows, rows), :], dist)
        for entry, dist, dst in base:
            mover.arrived(entry)
            for pos, far_dist in enumerate(far):
                mover.start(
                    dst.at[pl.ds(dist * rows, rows), pl.ds(0, blk)],
                    dst.at[pl.ds(dist * rows, rows), pl.ds((len(near) + pos) * blk, blk)],
                    0,
                    far_dist,
                )
        mover.finish()

    return run_exchange(
        body,
        (low, group_in, group_cot),
        [(rows * n_tok, low.shape[1]), (rows * n_tok, width), (rows * n_tok, width)],
        n_tok * (2 * (len(near) + len(far)) + 1),
        2,
    )


def slots_out(low_parts, out_parts, back_parts, rows, blk):
    n_tok, n_hid = lax.axis_size("tok"), lax.axis_size("hid")
    near, far = in_group_shifts(n_tok), hid_shifts(n_hid)

    def body(low_i, out_i, back_i, low_o, out_o, back_o, send, recv, held, kept):
        greet(
            [(dist, 0) for dist in range(1, n_tok)] + [(0, dist) for dist in far]
        )
        mover = Mover(send, recv)
        pairs = ((out_i, out_o), (back_i, back_o))
        waits = {}
        for dist in range(n_tok):
            for which, (src, _) in enumerate(pairs):
                for pos, far_dist in enumerate(far):
                    waits[dist, which, pos] = mover.start(
                        src.at[pl.ds(dist * rows, rows), pl.ds((len(near) + pos) * blk, blk)],
                        held.at[which, pos, pl.ds(dist * rows, rows), :],
                        0,
                        far_dist,
                    )
        for dist in range(n_tok):
            mover.start(low_i.at[pl.ds(dist * rows, rows), :], low_o.at[dist], dist)
        for pos in range(1, len(near)):
            for dist in range(n_tok):
                for src, dst in pairs:
                    mover.start(
                        src.at[pl.ds(dist * rows, rows), pl.ds(pos * blk, blk)],
                        dst.at[dist, pos],
                        dist,
                    )
        for dist in range(n_tok):
            for which, (src, dst) in enumerate(pairs):
                part = pl.ds(dist * rows, rows)
                total = src[part, pl.ds(0, blk)].astype(jnp.float32)
                for pos in range(len(far)):
                    mover.arrived(waits[dist, which, pos])
                    total = total + held[which, pos, part, :].astype(jnp.float32)
                kept[which, part, :] = total.astype(jnp.bfloat16)
                mover.start(kept.at[which, part, :], dst.at[dist, 0], dist)
        mover.finish()

    whole = rows * n_tok
    return run_exchange(
        body,
        (low_parts, out_parts, back_parts),
        [
            (n_tok, rows, low_parts.shape[1]),
            (n_tok, len(near), rows, blk),
            (n_tok, len(near), rows, blk),
        ],
        n_tok * (2 * (len(near) + len(far)) + 1),
        3,
        pltpu.VMEM,
        (
            pltpu.VMEM((2, len(far), whole, blk), jnp.bfloat16),
            pltpu.VMEM((2, whole, blk), jnp.bfloat16),
        ),
    )


def weights_out(low_sum, grad_first, grad_second):
    n_tok = lax.axis_size("tok")
    per, slots, whole, blk = grad_first.shape
    deep = whole // n_tok
    rows = low_sum.shape[0]

    def body(low_i, first, second, low_o, f_o, s_o, send, recv):
        me = lax.axis_index("tok")
        greet([(dist, 0) for dist in range(1, n_tok)])
        mover = Mover(send, recv)
        for dist in range(n_tok):
            mover.start(low_i, low_o.at[pl.ds(dist * rows, rows), :], dist)
        for dist in list(range(1, n_tok)) + [0]:
            for src, dst in ((first, f_o), (second, s_o)):
                mover.start(
                    src.at[:, :, span(me ^ dist, deep), :],
                    dst.at[span(me, per)],
                    dist,
                )
        mover.finish()

    shape = (per * n_tok, slots, deep, blk)
    return run_exchange(
        body,
        (low_sum, grad_first, grad_second),
        [(rows * n_tok, low_sum.shape[1]), shape, shape],
        3 * n_tok,
        4,
    )


def fetch_group(values, code, blk):
    n_tok = lax.axis_size("tok")
    whole = lax.all_gather(values, "hid", axis=0, tiled=False)
    group = lax.axis_index("hid") ^ (code // n_tok)
    rows = values.shape[0]
    return jnp.concatenate(
        [
            lax.dynamic_slice(
                whole, (group, 0, (place ^ (code % n_tok)) * blk), (1, rows, blk)
            )[0]
            for place in range(n_tok)
        ],
        axis=1,
    )


def return_group(got, code):
    n_tok = lax.axis_size("tok")
    me_tok = lax.axis_index("tok")
    shifts = in_group_shifts(n_tok)
    sums = []
    for place in range(n_tok):
        total = 0.0
        for pos, shift in enumerate(shifts):
            total = total + got[place ^ shift, pos].astype(jnp.float32)
        sums.append(total.astype(jnp.bfloat16))
    whole = lax.all_gather(jnp.stack(sums), "hid", axis=0, tiled=False)
    group = lax.axis_index("hid") ^ (code // n_tok)
    rows, blk = sums[0].shape
    return jnp.concatenate(
        [
            lax.dynamic_slice(
                whole, (group, me_tok ^ (code % n_tok) ^ place, 0, 0), (1, 1, rows, blk)
            )[0, 0]
            for place in range(n_tok)
        ],
        axis=1,
    )


def local_moved(
    tokens,
    in_blocks,
    in_left,
    in_right,
    in_lists,
    out_blocks,
    out_left,
    out_right,
    out_lists,
    cotangent,
):
    rows = tokens.shape[0]
    slots = in_blocks.shape[1]
    blk = in_blocks.shape[3]
    n_tok = lax.axis_size("tok")
    per = in_blocks.shape[0] // n_tok
    rank = in_left.shape[1]
    code_in = in_lists[0, 0]
    code_out = out_lists[0, 0]
    left_one, right_two, tok_own, cot_own, first, second = weights_in(
        tokens, cotangent, in_left, out_right, in_blocks, out_blocks
    )
    first = first.reshape(per, slots * blk, blk)
    group_in = fetch_group(tokens, code_in, blk)
    group_cot = fetch_group(cotangent, code_out, blk)
    own_in, own_back = rank_sum(
        (
            jnp.dot(tokens, left_one, preferred_element_type=jnp.float32),
            dot_cols(cotangent, right_two),
        )
    )
    own_low = jnp.concatenate(
        [own_in.astype(jnp.bfloat16), own_back.astype(jnp.bfloat16)], axis=1
    )
    low_all, x_in, x_cot = slots_in(own_low, group_in, group_cot, blk)
    low_in = low_all[:, :rank]
    low_back = low_all[:, rank:]

    preact = jnp.concatenate(
        [jnp.dot(x_in, first[at], preferred_element_type=jnp.float32) for at in range(per)],
        axis=1,
    ) + jnp.dot(low_in, in_right, preferred_element_type=jnp.float32)
    active, slopes = gelu_parts(preact)
    hidden = active.astype(jnp.bfloat16)
    hidden_q = [hidden[:, at * blk : (at + 1) * blk] for at in range(per)]
    grad_hidden = jnp.concatenate(
        [
            sum(
                dot_cols(x_cot[:, k * blk : (k + 1) * blk], second[at, k])
                for k in range(slots)
            )
            for at in range(per)
        ],
        axis=1,
    ) + dot_cols(low_back, out_left)
    grad_pre = (grad_hidden * slopes).astype(jnp.bfloat16)
    grad_q = [grad_pre[:, at * blk : (at + 1) * blk] for at in range(per)]

    low_parts = jnp.concatenate(
        [
            jnp.dot(hidden, out_left, preferred_element_type=jnp.float32),
            dot_cols(grad_pre, in_right),
        ],
        axis=1,
    ).astype(jnp.bfloat16)

    out_parts = jnp.concatenate(
        [
            sum(
                jnp.dot(hidden_q[at], second[at, k], preferred_element_type=jnp.float32)
                for at in range(per)
            )
            for k in range(slots)
        ],
        axis=1,
    )
    back_parts = sum(dot_cols(grad_q[at], first[at]) for at in range(per))
    low_got, out_got, back_got = slots_out(
        low_parts,
        out_parts.astype(jnp.bfloat16),
        back_parts.astype(jnp.bfloat16),
        rows,
        blk,
    )
    low_sum = rank_sum(
        sum(low_got[dist].astype(jnp.float32) for dist in range(n_tok))
    ).astype(jnp.bfloat16)
    low_mid = low_sum[:, :rank]
    low_grad = low_sum[:, rank:]
    sparse_out = return_group(out_got, code_out)
    sparse_back = return_group(back_got, code_in)
    layer_out = (
        sparse_out.astype(jnp.float32)
        + jnp.dot(low_mid, right_two, preferred_element_type=jnp.float32)
    ).astype(jnp.bfloat16)
    grad_tokens = (sparse_back.astype(jnp.float32) + dot_cols(low_grad, left_one)).astype(
        jnp.bfloat16
    )

    scale = lax.rsqrt(jnp.float32(rows * n_tok))
    grad_first = jnp.stack(
        [(scale * dot_rows(x_in, grad_q[at])).astype(jnp.bfloat16) for at in range(per)]
    ).reshape(per, slots, blk, blk)
    grad_second = jnp.stack(
        [
            jnp.stack(
                [
                    (scale * dot_rows(hidden_q[at], x_cot[:, k * blk : (k + 1) * blk])).astype(
                        jnp.bfloat16
                    )
                    for k in range(slots)
                ]
            )
            for at in range(per)
        ]
    )
    low_sum_all, grad_in_blocks, grad_out_blocks = weights_out(
        low_sum, grad_first, grad_second
    )
    return (
        layer_out,
        grad_tokens,
        grad_in_blocks,
        (scale * dot_rows(tok_own, low_sum_all[:, rank:])).astype(jnp.bfloat16),
        (scale * dot_rows(low_in, grad_pre)).astype(jnp.bfloat16),
        grad_out_blocks,
        (scale * dot_rows(hidden, low_back)).astype(jnp.bfloat16),
        (scale * dot_rows(low_sum_all[:, :rank], cot_own)).astype(jnp.bfloat16),
    )


def power_of_two(count):
    return count & (count - 1) == 0


def local(*arrays):
    tokens, in_blocks = arrays[0], arrays[1]
    n_tok = lax.axis_size("tok")
    n_hid = lax.axis_size("hid")
    whole_groups = (
        power_of_two(n_tok)
        and power_of_two(n_hid)
        and tokens.shape[1] == n_tok * in_blocks.shape[3]
        and in_blocks.shape[0] % n_tok == 0
    )
    return local_moved(*arrays) if whole_groups else local_gathered(*arrays)


def solution(mesh):
    return jax.shard_map(
        local,
        mesh=mesh,
        in_specs=(
            P("tok", "hid"),
            P("hid", None, "tok", None),
            P(("hid", "tok"), None),
            P(None, ("hid", "tok")),
            P(),
            P("hid", None, "tok", None),
            P(("hid", "tok"), None),
            P(None, ("hid", "tok")),
            P(),
            P("tok", "hid"),
        ),
        out_specs=(
            P("tok", "hid"),
            P("tok", "hid"),
            P("hid", None, "tok", None),
            P(("hid", "tok"), None),
            P(None, ("hid", "tok")),
            P("hid", None, "tok", None),
            P(("hid", "tok"), None),
            P(None, ("hid", "tok")),
        ),
        check_vma=False,
    )
```

```python
import jax
import jax.numpy as jnp
from jax import lax
from jax.experimental import pallas as pl
from jax.experimental.pallas import tpu as pltpu
from jax.sharding import PartitionSpec as P

D = 8192
BLK = 256


def gelu_parts(preact):
    inner_coef = 0.7978845608028654
    cubic_coef = 0.044715
    inner_arg = inner_coef * (preact + cubic_coef * preact * preact * preact)
    tanh_val = jnp.tanh(inner_arg)
    active = 0.5 * preact * (1.0 + tanh_val)
    slopes = 0.5 * (1.0 + tanh_val) + 0.5 * preact * (1.0 - tanh_val * tanh_val) * inner_coef * (
        1.0 + 3.0 * cubic_coef * preact * preact
    )
    return (active, slopes)


def dot_rows(left_arr, right_arr):
    return lax.dot_general(
        left_arr, right_arr, (((0,), (0,)), ((), ())), preferred_element_type=jnp.float32
    )


def dot_cols(left_arr, right_arr):
    return lax.dot_general(
        left_arr, right_arr, (((1,), (1,)), ((), ())), preferred_element_type=jnp.float32
    )


def rank_sum(values):
    return lax.psum(values, "hid")


def own_lists(lists, hid_blocks):
    return lax.dynamic_slice_in_dim(lists, lax.axis_index("hid") * hid_blocks, hid_blocks, 0)


def gather_in(values, lists, hid_blocks, blk_width):
    whole = lax.all_gather(values, "hid", axis=1, tiled=True)
    mine = own_lists(lists, hid_blocks)
    blocks = whole.reshape(whole.shape[0], whole.shape[1] // blk_width, blk_width)
    return blocks[:, mine.T]


def scatter_out(parts, lists, hid_blocks):
    mine = own_lists(lists, hid_blocks)
    picker = (mine.T[:, :, None] == jnp.arange(D // BLK, dtype=jnp.int32)[None, None, :]).astype(
        jnp.float32
    )
    dense = jnp.einsum("nsho,shc->nco", parts, picker, precision=lax.Precision.HIGHEST)
    return lax.psum_scatter(
        dense.reshape(dense.shape[0], -1), "hid", scatter_dimension=1, tiled=True
    )


def route_in(values, lists, hid_blocks, blk_width):
    return gather_in(values, lists, hid_blocks, blk_width)


def route_out(parts, lists, hid_blocks):
    return scatter_out(parts, lists, hid_blocks)


def local_gathered(
    tokens,
    in_blocks,
    in_left,
    in_right,
    in_lists,
    out_blocks,
    out_left,
    out_right,
    out_lists,
    cotangent,
):
    row_count, col_span = tokens.shape
    hid_blocks = in_blocks.shape[0]
    slot_count = in_blocks.shape[1]
    blk_width = in_blocks.shape[3]
    tok_count = lax.axis_size("tok")
    w_first, w_second, left_one, right_one, left_two, right_two = (
        lax.all_gather(in_blocks, "tok", axis=2, tiled=True),
        lax.all_gather(out_blocks, "tok", axis=2, tiled=True),
        lax.all_gather(in_left, "tok", axis=0, tiled=True),
        lax.all_gather(in_right, "tok", axis=1, tiled=True),
        lax.all_gather(out_left, "tok", axis=0, tiled=True),
        lax.all_gather(out_right, "tok", axis=1, tiled=True),
    )
    low_in, low_back = rank_sum(
        (
            jnp.dot(tokens, left_one, preferred_element_type=jnp.float32),
            dot_cols(cotangent, right_two),
        )
    )
    low_in = low_in.astype(jnp.bfloat16)
    low_back = low_back.astype(jnp.bfloat16)
    gathered = route_in(tokens, in_lists, hid_blocks, blk_width)
    group_count = gathered.shape[2]
    per_group = hid_blocks // group_count
    first_r = w_first.reshape(group_count, per_group, slot_count, blk_width, blk_width)
    second_r = w_second.reshape(group_count, per_group, slot_count, blk_width, blk_width)
    preact = jnp.einsum(
        "nseb,eqsbf->neqf", gathered, first_r, preferred_element_type=jnp.float32
    ).reshape(row_count, -1)
    preact = preact + jnp.dot(low_in, right_one, preferred_element_type=jnp.float32)
    active, slopes = gelu_parts(preact)
    hidden = active.astype(jnp.bfloat16)
    low_mid = rank_sum(jnp.dot(hidden, left_two, preferred_element_type=jnp.float32)).astype(
        jnp.bfloat16
    )
    hidden_r = hidden.reshape(row_count, group_count, per_group, blk_width)
    out_parts = jnp.einsum(
        "neqf,eqsfo->nseo", hidden_r, second_r, preferred_element_type=jnp.float32
    )
    sparse_out = route_out(out_parts, out_lists, hid_blocks)
    layer_out = (
        sparse_out + jnp.dot(low_mid, right_two, preferred_element_type=jnp.float32)
    ).astype(jnp.bfloat16)
    grad_in = route_in(cotangent, out_lists, hid_blocks, blk_width)
    grad_hidden = jnp.einsum(
        "nseo,eqsfo->neqf", grad_in, second_r, preferred_element_type=jnp.float32
    ).reshape(row_count, -1)
    grad_hidden = grad_hidden + dot_cols(low_back, left_two)
    grad_pre = (grad_hidden * slopes).astype(jnp.bfloat16)
    low_grad = rank_sum(dot_cols(grad_pre, right_one)).astype(jnp.bfloat16)
    grad_pre_r = grad_pre.reshape(row_count, group_count, per_group, blk_width)
    back_parts = jnp.einsum(
        "neqf,eqsbf->nseb", grad_pre_r, first_r, preferred_element_type=jnp.float32
    )
    sparse_back = route_out(back_parts, in_lists, hid_blocks)
    grad_tokens = (sparse_back + dot_cols(low_grad, left_one)).astype(jnp.bfloat16)
    loss_scale = lax.rsqrt(jnp.float32(row_count * tok_count))
    terms = (
        loss_scale
        * jnp.einsum(
            "nseb,neqf->eqsbf", gathered, grad_pre_r, preferred_element_type=jnp.float32
        ).reshape(w_first.shape),
        loss_scale
        * jnp.einsum(
            "neqf,nseo->eqsfo", hidden_r, grad_in, preferred_element_type=jnp.float32
        ).reshape(w_second.shape),
        loss_scale * dot_rows(tokens, low_grad),
        loss_scale * dot_rows(low_in, grad_pre),
        loss_scale * dot_rows(hidden, low_back),
        loss_scale * dot_rows(low_mid, cotangent),
    )
    shares = (
        lax.psum_scatter(
            terms[0].astype(jnp.bfloat16), "tok", scatter_dimension=2, tiled=True
        ).astype(jnp.float32),
        lax.psum_scatter(
            terms[1].astype(jnp.bfloat16), "tok", scatter_dimension=2, tiled=True
        ).astype(jnp.float32),
        lax.psum_scatter(
            terms[2].astype(jnp.bfloat16), "tok", scatter_dimension=0, tiled=True
        ).astype(jnp.float32),
        lax.psum_scatter(
            terms[3].astype(jnp.bfloat16), "tok", scatter_dimension=1, tiled=True
        ).astype(jnp.float32),
        lax.psum_scatter(
            terms[4].astype(jnp.bfloat16), "tok", scatter_dimension=0, tiled=True
        ).astype(jnp.float32),
        lax.psum_scatter(
            terms[5].astype(jnp.bfloat16), "tok", scatter_dimension=1, tiled=True
        ).astype(jnp.float32),
    )
    return (
        layer_out,
        grad_tokens,
        shares[0].astype(jnp.bfloat16),
        shares[2].astype(jnp.bfloat16),
        shares[3].astype(jnp.bfloat16),
        shares[1].astype(jnp.bfloat16),
        shares[4].astype(jnp.bfloat16),
        shares[5].astype(jnp.bfloat16),
    )


def in_group_shifts(count):
    return [0] + [1 << bit for bit in range(count.bit_length() - 1)]


def hid_shifts(count):
    return [1 << bit for bit in range(count.bit_length() - 1)]


def span(index, size):
    return pl.ds(pl.multiple_of(index * size, size), size)


def greet(partners):
    me_tok, me_hid = lax.axis_index("tok"), lax.axis_index("hid")
    barrier = pltpu.get_barrier_semaphore()
    for tok_dist, hid_dist in partners:
        pl.semaphore_signal(
            barrier,
            inc=1,
            device_id={"hid": me_hid ^ hid_dist, "tok": me_tok ^ tok_dist},
            device_id_type=pl.DeviceIdType.MESH,
        )
    pl.semaphore_wait(barrier, len(partners))


class Mover:
    def __init__(self, send, recv):
        self.send, self.recv, self.used = send, recv, 0
        self.open_copies = []

    def start(self, src, dst, tok_dist=0, hid_dist=0):
        at = self.used
        self.used += 1
        if tok_dist == 0 and hid_dist == 0:
            copy = pltpu.make_async_copy(src, dst, self.recv.at[at])
            copy.start()
            entry = [copy, True, False]
        else:
            copy = pltpu.make_async_remote_copy(
                src_ref=src,
                dst_ref=dst,
                send_sem=self.send.at[at],
                recv_sem=self.recv.at[at],
                device_id={
                    "hid": lax.axis_index("hid") ^ hid_dist,
                    "tok": lax.axis_index("tok") ^ tok_dist,
                },
                device_id_type=pl.DeviceIdType.MESH,
            )
            copy.start()
            entry = [copy, False, False]
        self.open_copies.append(entry)
        return entry

    def arrived(self, entry):
        if not entry[2]:
            if entry[1]:
                entry[0].wait()
            else:
                entry[0].wait_recv()
            entry[2] = True

    def finish(self):
        for entry in self.open_copies:
            self.arrived(entry)
        for entry in self.open_copies:
            if not entry[1]:
                entry[0].wait_send()


def double_sum(mover, far, totals, held):
    for pos, dist in enumerate(far):
        mover.arrived(mover.start(totals.at[pos], held.at[pos], 0, dist))
        totals[pos + 1] = totals[pos] + held[pos]
    return totals[len(far)]


def run_exchange(body, inputs, shapes, copies, ident, in_vmem=(), scratch=()):
    any_spec = pl.BlockSpec(memory_space=pl.ANY)
    return pl.pallas_call(
        body,
        out_shape=[jax.ShapeDtypeStruct(shape, jnp.bfloat16) for shape in shapes],
        in_specs=[
            pl.BlockSpec(memory_space=pltpu.VMEM) if at in in_vmem else any_spec
            for at in range(len(inputs))
        ],
        out_specs=[any_spec] * len(shapes),
        scratch_shapes=[
            pltpu.SemaphoreType.DMA((copies,)),
            pltpu.SemaphoreType.DMA((copies,)),
            *scratch,
        ],
        compiler_params=pltpu.CompilerParams(
            collective_id=ident, has_side_effects=True, vmem_limit_bytes=40 * 2**20
        ),
        cost_estimate=pl.CostEstimate(
            flops=0, bytes_accessed=200_000_000, transcendentals=0
        ),
    )(*inputs)


def weights_in(tokens, cotangent, in_left, out_right, in_blocks, out_blocks):
    n_tok = lax.axis_size("tok")
    rows, blk = tokens.shape[0], in_blocks.shape[3]
    hid_blocks, slots, deep, _ = in_blocks.shape
    per = hid_blocks // n_tok
    rank = in_left.shape[1]

    def body(tok, cot, left, right, first, second, left_o, right_o, tok_o, cot_o, f_o, s_o, send, recv):
        me = lax.axis_index("tok")
        greet([(dist, 0) for dist in range(1, n_tok)])
        mover = Mover(send, recv)
        for dist in range(n_tok):
            mover.start(left, left_o.at[span(me, blk), :], dist)
            mover.start(right, right_o.at[:, span(me, blk)], dist)
        for dist in list(range(1, n_tok)) + [0]:
            for src, dst in ((first, f_o), (second, s_o)):
                mover.start(
                    src.at[span(me ^ dist, per)],
                    dst.at[:, :, span(me, deep), :],
                    dist,
                )
        for dist in range(n_tok):
            for src, dst in ((tok, tok_o), (cot, cot_o)):
                mover.start(
                    src.at[:, span(me ^ dist, blk)], dst.at[pl.ds(dist * rows, rows), :], dist
                )
        mover.finish()

    full = (per, slots, deep * n_tok, blk)
    return run_exchange(
        body,
        (tokens, cotangent, in_left, out_right, in_blocks, out_blocks),
        [
            (blk * n_tok, rank),
            (rank, blk * n_tok),
            (rows * n_tok, blk),
            (rows * n_tok, blk),
            full,
            full,
        ],
        6 * n_tok,
        1,
    )


def slots_in(low, group_in, group_cot, blk):
    n_tok, n_hid = lax.axis_size("tok"), lax.axis_size("hid")
    rows = low.shape[0]
    near, far = in_group_shifts(n_tok), hid_shifts(n_hid)
    width = (len(near) + len(far)) * blk

    def body(low_i, in_i, cot_i, low_o, in_o, cot_o, send, recv, totals, held, low_sum):
        me = lax.axis_index("tok")
        greet(
            [(dist, 0) for dist in range(1, n_tok)] + [(0, dist) for dist in far]
        )
        mover = Mover(send, recv)
        pairs = ((in_i, in_o), (cot_i, cot_o))
        base = []
        for pos, shift in enumerate(near):
            for dist in range(n_tok):
                for src, dst in pairs:
                    entry = mover.start(
                        src.at[:, span(me ^ dist ^ shift, blk)],
                        dst.at[pl.ds(dist * rows, rows), pl.ds(pos * blk, blk)],
                        dist,
                    )
                    if pos == 0:
                        base.append((entry, dist, dst))
        totals[0] = low_i[...]
        low_sum[...] = double_sum(mover, far, totals, held).astype(jnp.bfloat16)
        for dist in range(n_tok):
            mover.start(low_sum, low_o.at[pl.ds(dist * rows, rows), :], dist)
        for entry, dist, dst in base:
            mover.arrived(entry)
            for pos, far_dist in enumerate(far):
                mover.start(
                    dst.at[pl.ds(dist * rows, rows), pl.ds(0, blk)],
                    dst.at[pl.ds(dist * rows, rows), pl.ds((len(near) + pos) * blk, blk)],
                    0,
                    far_dist,
                )
        mover.finish()

    return run_exchange(
        body,
        (low, group_in, group_cot),
        [(rows * n_tok, low.shape[1]), (rows * n_tok, width), (rows * n_tok, width)],
        n_tok * (2 * (len(near) + len(far)) + 1) + len(far),
        2,
        (0,),
        (
            pltpu.VMEM((len(far) + 1,) + low.shape, jnp.float32),
            pltpu.VMEM((len(far),) + low.shape, jnp.float32),
            pltpu.VMEM(low.shape, jnp.bfloat16),
        ),
    )


def slots_out(low_parts, out_parts, back_parts, rows, blk):
    n_tok, n_hid = lax.axis_size("tok"), lax.axis_size("hid")
    near, far = in_group_shifts(n_tok), hid_shifts(n_hid)

    def body(
        low_i, out_i, back_i, low_o, out_o, back_o, send, recv,
        held, kept, low_got, totals, low_held, low_sum,
    ):
        greet(
            [(dist, 0) for dist in range(1, n_tok)] + [(0, dist) for dist in far]
        )
        mover = Mover(send, recv)
        pairs = ((out_i, out_o), (back_i, back_o))
        waits = {}
        for dist in range(n_tok):
            for which, (src, _) in enumerate(pairs):
                for pos, far_dist in enumerate(far):
                    waits[dist, which, pos] = mover.start(
                        src.at[pl.ds(dist * rows, rows), pl.ds((len(near) + pos) * blk, blk)],
                        held.at[which, pos, pl.ds(dist * rows, rows), :],
                        0,
                        far_dist,
                    )
        lows = [
            mover.start(low_i.at[pl.ds(dist * rows, rows), :], low_got.at[dist], dist)
            for dist in range(n_tok)
        ]
        for pos in range(1, len(near)):
            for dist in range(n_tok):
                for src, dst in pairs:
                    mover.start(
                        src.at[pl.ds(dist * rows, rows), pl.ds(pos * blk, blk)],
                        dst.at[dist, pos],
                        dist,
                    )
        for dist in range(n_tok):
            for which, (src, dst) in enumerate(pairs):
                part = pl.ds(dist * rows, rows)
                total = src[part, pl.ds(0, blk)].astype(jnp.float32)
                for pos in range(len(far)):
                    mover.arrived(waits[dist, which, pos])
                    total = total + held[which, pos, part, :].astype(jnp.float32)
                kept[which, part, :] = total.astype(jnp.bfloat16)
                mover.start(kept.at[which, part, :], dst.at[dist, 0], dist)
        for entry in lows:
            mover.arrived(entry)
        totals[0] = sum(low_got[dist].astype(jnp.float32) for dist in range(n_tok))
        low_sum[...] = double_sum(mover, far, totals, low_held).astype(jnp.bfloat16)
        for dist in range(n_tok):
            mover.start(low_sum, low_o.at[pl.ds(dist * rows, rows), :], dist)
        mover.finish()

    whole = rows * n_tok
    width = low_parts.shape[1]
    return run_exchange(
        body,
        (low_parts, out_parts, back_parts),
        [
            (whole, width),
            (n_tok, len(near), rows, blk),
            (n_tok, len(near), rows, blk),
        ],
        n_tok * (2 * (len(near) + len(far)) + 2) + len(far),
        3,
        (0, 1, 2),
        (
            pltpu.VMEM((2, len(far), whole, blk), jnp.bfloat16),
            pltpu.VMEM((2, whole, blk), jnp.bfloat16),
            pltpu.VMEM((n_tok, rows, width), jnp.bfloat16),
            pltpu.VMEM((len(far) + 1, rows, width), jnp.float32),
            pltpu.VMEM((len(far), rows, width), jnp.float32),
            pltpu.VMEM((rows, width), jnp.bfloat16),
        ),
    )


def weights_out(grad_first, grad_second):
    n_tok = lax.axis_size("tok")
    per, slots, whole, blk = grad_first.shape
    deep = whole // n_tok

    def body(first, second, f_o, s_o, send, recv):
        me = lax.axis_index("tok")
        greet([(dist, 0) for dist in range(1, n_tok)])
        mover = Mover(send, recv)
        for dist in list(range(1, n_tok)) + [0]:
            for src, dst in ((first, f_o), (second, s_o)):
                mover.start(
                    src.at[:, :, span(me ^ dist, deep), :],
                    dst.at[span(me, per)],
                    dist,
                )
        mover.finish()

    shape = (per * n_tok, slots, deep, blk)
    return run_exchange(
        body,
        (grad_first, grad_second),
        [shape, shape],
        2 * n_tok,
        4,
    )


def fetch_group(values, code, blk):
    n_tok = lax.axis_size("tok")
    whole = lax.all_gather(values, "hid", axis=0, tiled=False)
    group = lax.axis_index("hid") ^ (code // n_tok)
    rows = values.shape[0]
    return jnp.concatenate(
        [
            lax.dynamic_slice(
                whole, (group, 0, (place ^ (code % n_tok)) * blk), (1, rows, blk)
            )[0]
            for place in range(n_tok)
        ],
        axis=1,
    )


def return_group(got, code):
    n_tok = lax.axis_size("tok")
    me_tok = lax.axis_index("tok")
    shifts = in_group_shifts(n_tok)
    sums = []
    for place in range(n_tok):
        total = 0.0
        for pos, shift in enumerate(shifts):
            total = total + got[place ^ shift, pos].astype(jnp.float32)
        sums.append(total.astype(jnp.bfloat16))
    whole = lax.all_gather(jnp.stack(sums), "hid", axis=0, tiled=False)
    group = lax.axis_index("hid") ^ (code // n_tok)
    rows, blk = sums[0].shape
    return jnp.concatenate(
        [
            lax.dynamic_slice(
                whole, (group, me_tok ^ (code % n_tok) ^ place, 0, 0), (1, 1, rows, blk)
            )[0, 0]
            for place in range(n_tok)
        ],
        axis=1,
    )


def local_moved(
    tokens,
    in_blocks,
    in_left,
    in_right,
    in_lists,
    out_blocks,
    out_left,
    out_right,
    out_lists,
    cotangent,
):
    rows = tokens.shape[0]
    slots = in_blocks.shape[1]
    blk = in_blocks.shape[3]
    n_tok = lax.axis_size("tok")
    per = in_blocks.shape[0] // n_tok
    rank = in_left.shape[1]
    code_in = in_lists[0, 0]
    code_out = out_lists[0, 0]
    left_one, right_two, tok_own, cot_own, first, second = weights_in(
        tokens, cotangent, in_left, out_right, in_blocks, out_blocks
    )
    first = first.reshape(per, slots * blk, blk)
    group_in = fetch_group(tokens, code_in, blk)
    group_cot = fetch_group(cotangent, code_out, blk)
    own_low = jnp.concatenate(
        [
            jnp.dot(tokens, left_one, preferred_element_type=jnp.float32),
            dot_cols(cotangent, right_two),
        ],
        axis=1,
    )
    low_all, x_in, x_cot = slots_in(own_low, group_in, group_cot, blk)
    low_in = low_all[:, :rank]
    low_back = low_all[:, rank:]

    preact = jnp.concatenate(
        [jnp.dot(x_in, first[at], preferred_element_type=jnp.float32) for at in range(per)],
        axis=1,
    ) + jnp.dot(low_in, in_right, preferred_element_type=jnp.float32)
    active, slopes = gelu_parts(preact)
    hidden = active.astype(jnp.bfloat16)
    hidden_q = [hidden[:, at * blk : (at + 1) * blk] for at in range(per)]
    grad_hidden = jnp.concatenate(
        [
            sum(
                dot_cols(x_cot[:, k * blk : (k + 1) * blk], second[at, k])
                for k in range(slots)
            )
            for at in range(per)
        ],
        axis=1,
    ) + dot_cols(low_back, out_left)
    grad_pre = (grad_hidden * slopes).astype(jnp.bfloat16)
    grad_q = [grad_pre[:, at * blk : (at + 1) * blk] for at in range(per)]

    low_parts = jnp.concatenate(
        [
            jnp.dot(hidden, out_left, preferred_element_type=jnp.float32),
            dot_cols(grad_pre, in_right),
        ],
        axis=1,
    ).astype(jnp.bfloat16)

    out_parts = jnp.concatenate(
        [
            sum(
                jnp.dot(hidden_q[at], second[at, k], preferred_element_type=jnp.float32)
                for at in range(per)
            )
            for k in range(slots)
        ],
        axis=1,
    )
    back_parts = sum(dot_cols(grad_q[at], first[at]) for at in range(per))
    low_sum_all, out_got, back_got = slots_out(
        low_parts,
        out_parts.astype(jnp.bfloat16),
        back_parts.astype(jnp.bfloat16),
        rows,
        blk,
    )
    low_sum = low_sum_all[:rows]
    low_mid = low_sum[:, :rank]
    low_grad = low_sum[:, rank:]
    sparse_out = return_group(out_got, code_out)
    sparse_back = return_group(back_got, code_in)
    layer_out = (
        sparse_out.astype(jnp.float32)
        + jnp.dot(low_mid, right_two, preferred_element_type=jnp.float32)
    ).astype(jnp.bfloat16)
    grad_tokens = (sparse_back.astype(jnp.float32) + dot_cols(low_grad, left_one)).astype(
        jnp.bfloat16
    )

    scale = lax.rsqrt(jnp.float32(rows * n_tok))
    grad_first = jnp.stack(
        [(scale * dot_rows(x_in, grad_q[at])).astype(jnp.bfloat16) for at in range(per)]
    ).reshape(per, slots, blk, blk)
    grad_second = jnp.stack(
        [
            jnp.stack(
                [
                    (scale * dot_rows(hidden_q[at], x_cot[:, k * blk : (k + 1) * blk])).astype(
                        jnp.bfloat16
                    )
                    for k in range(slots)
                ]
            )
            for at in range(per)
        ]
    )
    grad_in_blocks, grad_out_blocks = weights_out(grad_first, grad_second)
    return (
        layer_out,
        grad_tokens,
        grad_in_blocks,
        (scale * dot_rows(tok_own, low_sum_all[:, rank:])).astype(jnp.bfloat16),
        (scale * dot_rows(low_in, grad_pre)).astype(jnp.bfloat16),
        grad_out_blocks,
        (scale * dot_rows(hidden, low_back)).astype(jnp.bfloat16),
        (scale * dot_rows(low_sum_all[:, :rank], cot_own)).astype(jnp.bfloat16),
    )


def power_of_two(count):
    return count & (count - 1) == 0


def local(*arrays):
    tokens, in_blocks = arrays[0], arrays[1]
    n_tok = lax.axis_size("tok")
    n_hid = lax.axis_size("hid")
    whole_groups = (
        power_of_two(n_tok)
        and power_of_two(n_hid)
        and tokens.shape[1] == n_tok * in_blocks.shape[3]
        and in_blocks.shape[0] % n_tok == 0
    )
    return local_moved(*arrays) if whole_groups else local_gathered(*arrays)


def solution(mesh):
    return jax.shard_map(
        local,
        mesh=mesh,
        in_specs=(
            P("tok", "hid"),
            P("hid", None, "tok", None),
            P(("hid", "tok"), None),
            P(None, ("hid", "tok")),
            P(),
            P("hid", None, "tok", None),
            P(("hid", "tok"), None),
            P(None, ("hid", "tok")),
            P(),
            P("tok", "hid"),
        ),
        out_specs=(
            P("tok", "hid"),
            P("tok", "hid"),
            P("hid", None, "tok", None),
            P(("hid", "tok"), None),
            P(None, ("hid", "tok")),
            P("hid", None, "tok", None),
            P(("hid", "tok"), None),
            P(None, ("hid", "tok")),
        ),
        check_vma=False,
    )
```
